32 devices in a mesh: exp: 4 (over y, x), dp: 8 (over z, core).
Axes of the slice: x: 2, y: 2, z: 4, core: 2. Of those that a mesh axis runs over, the one named last changes fastest.
Arguments:
- expert_inputs: bfloat16 [4, 2048, 2048], P('exp', 'dp'), may hold values from -6 to 6
- hidden_grads: bfloat16 [4, 2048, 7168], P('exp', 'dp'), may hold values from -0.125 to 0.125
- expert_weight: float32 [4, 2048, 7168], P('exp', 'dp'), may hold values from -0.125 to 0.125
- expert_moment: bfloat16 [4, 2048, 7168], P('exp', 'dp'), may hold values from -4 to 4
- expert_second: bfloat16 [4, 2048, 7168], P('exp', 'dp'), may hold values from 0.0009994507 to 1
- key_partial: float32 [4, 2048, 512], P('exp', 'dp'), may hold values from -5 to 5
- key_weight: float32 [2048, 512], P('dp'), may hold values from -0.125 to 0.125
- key_moment: float32 [4, 512, 512], P('exp', 'dp'), may hold values from -4 to 4
- key_second: float32 [4, 512, 512], P('exp', 'dp'), may hold values from 0.001 to 1
- slice_owner: int32 [4], replicated, may hold values from 0 to 3, each once
Outputs:
- expert_weight_next: float32 [4, 2048, 7168], P('exp', 'dp')
- expert_moment_next: bfloat16 [4, 2048, 7168], P('exp', 'dp')
- expert_second_next: bfloat16 [4, 2048, 7168], P('exp', 'dp')
- key_weight_next: float32 [2048, 512], P('dp')
- key_moment_next: float32 [4, 512, 512], P('exp', 'dp')
- key_second_next: float32 [4, 512, 512], P('exp', 'dp')
The draws below stay inside these ranges and needn't reach their ends.
Inputs may be any that keep to these rules, and one draw needn't show every extreme that they name: `slice_owner`: each exp group holds exactly one slice.
All inputs are finite; a program needn't handle non-finite values.
Results may differ from the reference program's by a relative error of at most 0.012.
Values may be sent and summed in bfloat16 or wider, within the bound.
A program may use at most 192 MiB of HBM per device.

```python
import math
import jax
import jax.numpy as jnp
from jax import lax

DW = 2048
FE = 7168
KA = 512
TOK_DEV = 256
STEP = 10
TOKENS = 2048
N_EXP = 4
N_DP = 8


def strengthened(values, key, source, target, blocks, factor):
    def block_of(position):
        return (jnp.arange(values.shape[position]) // (values.shape[position] // blocks)).reshape((-1,) + (1,) * (values.ndim - 1 - position))

    one_side = jax.random.permutation(key, blocks)[block_of(target)]
    far = (block_of(target) + blocks // 2) % blocks
    return jnp.where((block_of(source) == one_side) | (block_of(source) == far), factor * values, values)


def block_scale(rng, shape, shards, low, high):
    factor_of = 1.0
    for axis_at, parts in shards:
        heights = jax.random.uniform(jax.random.fold_in(jax.random.fold_in(rng, 6), axis_at), (parts,), jnp.float32, low / len(shards), high / len(shards))
        factor_of = factor_of * jnp.repeat(jnp.exp(heights), shape[axis_at] // parts).reshape((-1,) + (1,) * (len(shape) - 1 - axis_at))
    return factor_of


def bell_draw(key, dims, deviation, reach, shards=(), kind=jnp.bfloat16):
    factor_of = block_scale(key, dims, shards, -0.22, 0.18) if shards else 1.0
    array = jax.random.normal(key, dims, jnp.float32) * deviation * factor_of
    return jnp.minimum(jnp.maximum(array, -reach), reach).astype(kind)


def gaussian_with(own_key, extent, width, reach, cuts, heavy, kind=jnp.bfloat16):
    entries = width * jax.random.normal(own_key, extent, jnp.float32)
    if cuts:
        entries = entries * block_scale(own_key, extent, cuts, -0.22, 0.18)
    return jnp.clip(strengthened(entries, jax.random.fold_in(own_key, 3), *heavy), -reach, reach).astype(kind)


def setup_inputs(seed: int = 0) -> dict:
    key_of = jax.random.split(jax.random.key(seed), 11)
    return {
        "expert_inputs": gaussian_with(key_of[0], (N_EXP, TOKENS, DW), 1.0, 6.0, ((0, 4), (1, 8)), (1, 2, 8, 2.0)),
        "hidden_grads": bell_draw(key_of[1], (N_EXP, TOKENS, FE), TOKENS ** -0.5, 0.125, ((0, 4), (1, 8))),
        "expert_weight": bell_draw(key_of[2], (N_EXP, DW, FE), DW ** -0.5, 0.125, ((0, 4), (1, 8)), jnp.float32),
        "expert_moment": bell_draw(key_of[3], (N_EXP, DW, FE), 0.3, 4.0, ((0, 4), (1, 8))),
        "expert_second": jnp.clip(jnp.exp(math.log(1.0) - 6.9083047 * jax.random.uniform(key_of[4], (N_EXP, DW, FE), jnp.float32) ** block_scale(key_of[4], (N_EXP, DW, FE), ((0, 4), (1, 8)), -0.2, 0.2)), 0.0009994507, 1.0).astype(jnp.bfloat16),
        "key_partial": bell_draw(key_of[5], (N_EXP, DW, KA), 0.35, 5.0, ((0, 4), (1, 8)), jnp.float32),
        "key_weight": bell_draw(key_of[6], (DW, KA), DW ** -0.5, 0.125, ((0, 8),), jnp.float32),
        "key_moment": bell_draw(key_of[7], (N_EXP, DW // N_EXP, KA), 0.3, 4.0, ((0, 4), (1, 8)), jnp.float32),
        "key_second": jnp.clip(jnp.exp(math.log(1.0) - 6.9077552 * jax.random.uniform(key_of[8], (N_EXP, DW // N_EXP, KA), jnp.float32) ** block_scale(key_of[8], (N_EXP, DW // N_EXP, KA), ((0, 4), (1, 8)), -0.2, 0.2)), 0.001, 1.0),
        "slice_owner": jax.random.permutation(key_of[9], N_EXP).astype(jnp.int32),
    }


first_decay = 0.9
second_decay = 0.999
learn_rate = 0.01
weight_decay = 0.1
epsilon = 1e-08

def adam_update(param, moment, second, gradient):
    moment_new = first_decay * moment.astype(jnp.float32) + (1.0 - first_decay) * gradient
    second_new = second_decay * second.astype(jnp.float32) + (1.0 - second_decay) * gradient * gradient
    moment_hat = moment_new / (1.0 - first_decay ** STEP)
    second_hat = second_new / (1.0 - second_decay ** STEP)
    param_new = param - learn_rate * (moment_hat / (jnp.sqrt(second_hat) + epsilon) + weight_decay * param)
    return (param_new, moment_new, second_new)

def one_expert(packed):
    inputs, upstream, param, moment, second = packed

    def accumulate(running, block):
        offset = (block * TOK_DEV).astype(jnp.int32)
        rows_in = lax.dynamic_slice_in_dim(inputs, offset, TOK_DEV, 0)
        rows_up = lax.dynamic_slice_in_dim(upstream, offset, TOK_DEV, 0)
        partial_value = lax.dot_general(rows_in, rows_up, (((0,), (0,)), ((), ())), preferred_element_type=jnp.float32)
        partial_value = lax.optimization_barrier(partial_value.astype(jnp.bfloat16)).astype(jnp.float32)
        return (running + partial_value, None)
    gradient, _ = lax.scan(accumulate, jnp.zeros((DW, FE), jnp.float32), jnp.arange(N_DP, dtype=jnp.int32))
    param_new, moment_new, second_new = adam_update(param, moment, second, gradient)
    return (param_new, moment_new.astype(jnp.bfloat16), second_new.astype(jnp.bfloat16))

def reference(expert_inputs, hidden_grads, expert_weight, expert_moment, expert_second, key_partial, key_weight, key_moment, key_second, slice_owner):
    expert_weight_next, expert_moment_next, expert_second_next = lax.map(one_expert, (expert_inputs, hidden_grads, expert_weight, expert_moment, expert_second))
    slice_rows = DW // (N_DP * N_EXP)
    key_gradient = lax.optimization_barrier(jnp.sum(key_partial, axis=0))
    owner = slice_owner.astype(jnp.int32)

    def to_rows(held):
        ordered = held.reshape(N_EXP, N_DP, slice_rows, KA)[owner]
        return jnp.transpose(ordered, (1, 0, 2, 3)).reshape(DW, KA)
    inverse = jnp.zeros((N_EXP,), jnp.int32).at[owner].set(jnp.arange(N_EXP, dtype=jnp.int32))

    def to_held(rows):
        ordered = jnp.transpose(rows.reshape(N_DP, N_EXP, slice_rows, KA), (1, 0, 2, 3))
        return ordered[inverse].reshape(N_EXP, DW // N_EXP, KA)
    key_weight_next, moment_rows, second_rows = adam_update(key_weight, to_rows(key_moment), to_rows(key_second), key_gradient)
    return (expert_weight_next, expert_moment_next, expert_second_next, key_weight_next, to_held(moment_rows), to_held(second_rows))
```

```python
import functools

import jax
import jax.numpy as jnp
from jax import lax
from jax.experimental import pallas as pl
from jax.experimental.pallas import tpu as pltpu
from jax.sharding import PartitionSpec as P

STEP = 10


first_decay = 0.9
second_decay = 0.999
learn_rate = 0.01
weight_decay = 0.1
epsilon = 1e-08


def adam_update(param, moment, second, gradient):
    moment_new = first_decay * moment.astype(jnp.float32) + (1.0 - first_decay) * gradient
    second_new = (
        second_decay * second.astype(jnp.float32) + (1.0 - second_decay) * gradient * gradient
    )
    moment_hat = moment_new / (1.0 - first_decay**STEP)
    second_hat = second_new / (1.0 - second_decay**STEP)
    param_new = param - learn_rate * (
        moment_hat / (jnp.sqrt(second_hat) + epsilon) + weight_decay * param
    )
    return (param_new, moment_new, second_new)


def shards(
    expert_inputs,
    hidden_grads,
    expert_weight,
    expert_moment,
    expert_second,
    key_partial,
    key_weight,
    key_moment,
    key_second,
    slice_owner,
):
    inputs = expert_inputs[0]
    upstream = hidden_grads[0]
    gradient = lax.psum_scatter(
        lax.dot_general(
            inputs, upstream, (((0,), (0,)), ((), ())), preferred_element_type=jnp.float32
        ).astype(jnp.bfloat16),
        "dp",
        scatter_dimension=0,
        tiled=True,
    ).astype(jnp.float32)
    weight_next, moment_f, second_f = adam_update(
        expert_weight[0], expert_moment[0], expert_second[0], gradient
    )
    moment_next = moment_f.astype(jnp.bfloat16)
    second_next = second_f.astype(jnp.bfloat16)
    groups = lax.axis_size("exp")
    holder = lax.axis_index("exp")
    shard_rows = key_weight.shape[0]
    slice_rows = shard_rows // groups
    columns_key = key_weight.shape[1]
    picker = (slice_owner[None, :] == jnp.arange(groups, dtype=jnp.int32)[:, None]).astype(
        jnp.float32
    )
    flat_partial = key_partial[0].reshape(groups, slice_rows * columns_key)
    arranged = jnp.dot(
        picker, flat_partial, precision=lax.Precision.HIGHEST, preferred_element_type=jnp.float32
    )
    key_gradient = (
        lax.psum_scatter(arranged.astype(jnp.bfloat16), "exp", scatter_dimension=0, tiled=True)
        .astype(jnp.float32)
        .reshape(slice_rows, columns_key)
    )
    held_slice = jnp.sum(jnp.where(slice_owner == holder, jnp.arange(groups, dtype=jnp.int32), 0))
    old_slice = lax.dynamic_slice_in_dim(key_weight, held_slice * slice_rows, slice_rows, 0)
    slice_new, key_moment_new, key_second_new = adam_update(
        old_slice, key_moment[0], key_second[0], key_gradient
    )
    gathered = lax.all_gather(slice_new, "exp", axis=0, tiled=True).reshape(
        groups, slice_rows * columns_key
    )
    ordered = jnp.dot(
        picker.T, gathered, precision=lax.Precision.HIGHEST, preferred_element_type=jnp.float32
    )
    key_next = ordered.reshape(shard_rows, columns_key)
    return (
        weight_next[None],
        moment_next[None],
        second_next[None],
        key_next,
        key_moment_new[None],
        key_second_new[None],
    )


MESH = pl.DeviceIdType.MESH
CHAIN = 4


def kernel(
    chunk,
    in_ref,
    hid_ref,
    karr_ref,
    kold_ref,
    kmom_ref,
    ksec_ref,
    g_ref,
    kall_ref,
    kmom_out,
    ksec_out,
    lhs,
    rhs,
    prod,
    got,
    fwd,
    own,
    kgot,
    local_sem,
    swap_send,
    swap_recv,
    fact_send,
    fact_recv,
    far_send,
    far_recv,
    near_send,
    near_recv,
    out_sem,
    out_send,
    out_recv,
    lhs_send,
    lhs_recv,
    edge_send,
    edge_recv,
    pass_send,
    pass_recv,
    key_send,
    key_recv,
    all_send,
    all_recv,
):
    exp = lax.axis_index("exp")
    groups = lax.axis_size("exp")
    place = lax.axis_index("dp")
    chip = place // 2
    core = place % 2
    other = 1 - core
    partner = (exp, chip * 2 + other)
    tokens, width = in_ref.shape
    rows = width // (2 * CHAIN)
    block = 2 * rows
    half = hid_ref.shape[1] // 2
    count = half // chunk
    middle = (chip == 1) | (chip == 2)
    outer = (chip // 2) * (CHAIN - 1)
    far = CHAIN - 1 - outer
    inner = 1 + (1 - chip // 2)
    near = 1 + chip // 2
    outer_dev = (exp, outer * 2 + core)
    inner_dev = (exp, inner * 2 + core)
    near_dev = (exp, near * 2 + core)

    def remote(src, dst, send, recv, dev):
        return pltpu.make_async_remote_copy(
            src_ref=src, dst_ref=dst, send_sem=send, recv_sem=recv, device_id=dev,
            device_id_type=MESH,
        )

    def rows_of(which):
        return pl.ds(pl.multiple_of(which * block, block), block)

    def columns(side, c):
        return pl.ds(pl.multiple_of(side * half + c * chunk, chunk), chunk)

    def matmul(which, c, depth):
        return jnp.dot(
            lhs[rows_of(which), 0:depth], rhs[c, 0:depth, :], preferred_element_type=jnp.float32
        )

    def local_copy(c):
        return pltpu.make_async_copy(
            hid_ref.at[:, columns(core, c)], rhs.at[c, pl.ds(0, tokens)], local_sem.at[c]
        )

    def swap_copy(c):
        return remote(
            hid_ref.at[:, columns(other, c)], rhs.at[c, pl.ds(tokens, tokens)],
            swap_send.at[c], swap_recv.at[c], partner,
        )

    def factor_copy(c):
        return remote(
            rhs.at[c, pl.ds(0, 2 * tokens)], rhs.at[c, pl.ds(2 * tokens, 2 * tokens)],
            fact_send.at[c], fact_recv.at[c], near_dev,
        )

    def far_copy(c):
        return remote(
            prod.at[c, pl.ds(0, block)], got.at[c, pl.ds(0, block)],
            far_send.at[c], far_recv.at[c], inner_dev,
        )

    def near_copy(c):
        return remote(
            prod.at[c, pl.ds(block, block)], got.at[c, pl.ds(block, block)],
            near_send.at[c], near_recv.at[c], inner_dev,
        )

    def edge_result(c):
        return remote(
            fwd.at[c], got.at[c, pl.ds(block, block)], far_recv_send(c), near_recv.at[c], outer_dev
        )

    def far_recv_send(c):
        return fact_send.at[c]

    def out_copy(c):
        return pltpu.make_async_copy(
            own.at[c, pl.ds(pl.multiple_of(core * rows, rows), rows)],
            g_ref.at[:, columns(core, c)], out_sem.at[c],
        )

    def out_swap(c):
        return remote(
            own.at[c, pl.ds(pl.multiple_of(other * rows, rows), rows)],
            g_ref.at[:, columns(core, c)], out_send.at[c], out_recv.at[c], partner,
        )

    lhs_swap = remote(
        lhs.at[:, pl.ds(0, tokens)], lhs.at[:, pl.ds(tokens, tokens)],
        lhs_send, lhs_recv, partner,
    )

    def part_of(k):
        return (far, inner, near)[k]

    def edge_copy(k):
        at = rows_of(part_of(k))
        return remote(
            lhs.at[at, pl.ds(0, tokens)], lhs.at[at, pl.ds(2 * tokens, tokens)],
            edge_send.at[k], edge_recv.at[k], near_dev,
        )

    def pass_copy(k):
        at = rows_of(part_of(k))
        return remote(
            lhs.at[at, pl.ds(2 * tokens, tokens)], lhs.at[at, pl.ds(3 * tokens, tokens)],
            pass_send.at[k], pass_recv.at[k], partner,
        )

    def key_copy(d):
        peer = lax.rem(exp + d, groups)
        return remote(
            karr_ref.at[peer], kgot.at[d - 1], key_send.at[d - 1], key_recv.at[d - 1],
            (peer, place),
        )

    def all_copy(d):
        peer = lax.rem(exp + d, groups)
        return remote(
            kall_ref.at[exp], kall_ref.at[exp], all_send.at[d - 1], all_recv.at[d - 1],
            (peer, place),
        )

    def all_arrival(d):
        source = lax.rem(exp + groups - d, groups)
        return remote(
            kall_ref.at[source], kall_ref.at[source], all_send.at[d - 1], all_recv.at[d - 1],
            (source, place),
        )

    barrier = pltpu.get_barrier_semaphore()

    def greet(dev):
        pl.semaphore_signal(barrier, inc=1, device_id=dev, device_id_type=MESH)

    greet(partner)
    for d in range(1, groups):
        greet((lax.rem(exp + d, groups), place))

    @pl.when(middle)
    def _():
        greet(outer_dev)
        greet(inner_dev)
        pl.semaphore_wait(barrier, groups + 2)

    @pl.when(jnp.logical_not(middle))
    def _():
        greet(near_dev)
        pl.semaphore_wait(barrier, groups + 1)

    @pl.loop(0, count)
    def _(c):
        local_copy(c).start()
        swap_copy(c).start()

    @pl.loop(0, 2 * CHAIN)
    def _(q):
        at = pl.ds(pl.multiple_of(q * rows, rows), rows)
        lhs[at, 0:tokens] = in_ref[:, at].T

    @pl.when(jnp.logical_not(middle))
    def _():
        for k in range(3):
            edge_copy(k).start()

    lhs_swap.start()
    for d in range(1, groups):
        key_copy(d).start()

    def key_step():
        for d in range(1, groups):
            key_copy(d).wait_recv()
        total = karr_ref[exp].astype(jnp.float32)
        for d in range(1, groups):
            total += kgot[d - 1].astype(jnp.float32)
        new, moment, second = adam_update(kold_ref[...], kmom_ref[...], ksec_ref[...], total)
        kmom_out[...] = moment
        ksec_out[...] = second
        kall_ref[exp] = new
        for d in range(1, groups):
            all_copy(d).start()

    def finish(c, depth):
        own[c] = (matmul(chip, c, depth) + got[c, block:, :].astype(jnp.float32)).astype(own.dtype)
        out_copy(c).start()
        out_swap(c).start()

    @pl.when(jnp.logical_not(middle))
    def _():
        @pl.loop(0, count)
        def _(c):
            local_copy(c).wait()
            swap_copy(c).wait_recv()
            factor_copy(c).start()

        lhs_swap.wait_recv()
        key_step()

        @pl.loop(0, count)
        def _(c):
            near_copy(c).wait_recv()
            finish(c, 2 * tokens)

        @pl.loop(0, count)
        def _(c):
            factor_copy(c).wait_send()

        for k in range(3):
            edge_copy(k).wait_send()

    @pl.when(middle)
    def _():
        for k in range(3):
            edge_copy(k).wait_recv()
            pass_copy(k).start()
        lhs_swap.wait_recv()
        for k in range(3):
            pass_copy(k).wait_recv()

        @pl.loop(0, count + 1)
        def _(c):
            @pl.when(c < count)
            def _():
                local_copy(c).wait()
                swap_copy(c).wait_recv()
                factor_copy(c).wait_recv()
                prod[c, 0:block, :] = matmul(far, c, 4 * tokens).astype(prod.dtype)
                far_copy(c).start()
                prod[c, block:, :] = matmul(inner, c, 4 * tokens).astype(prod.dtype)
                near_copy(c).start()

            @pl.when(c == 1)
            def _():
                key_step()

            @pl.when(c > 0)
            def _():
                p = c - 1
                far_copy(p).wait_recv()
                fwd[p] = (
                    matmul(outer, p, 2 * tokens) + got[p, 0:block, :].astype(jnp.float32)
                ).astype(fwd.dtype)
                edge_result(p).start()
                near_copy(p).wait_recv()
                finish(p, 4 * tokens)

        @pl.loop(0, count)
        def _(c):
            far_copy(c).wait_send()
            near_copy(c).wait_send()
            edge_result(c).wait_send()

        for k in range(3):
            pass_copy(k).wait_send()

    lhs_swap.wait_send()
    for d in range(1, groups):
        key_copy(d).wait_send()
        all_copy(d).wait_send()
        all_arrival(d).wait_recv()

    @pl.loop(0, count)
    def _(c):
        swap_copy(c).wait_send()
        out_copy(c).wait()
        out_swap(c).wait_send()
        remote(
            own.at[c, pl.ds(0, rows)], g_ref.at[:, columns(other, c)],
            out_send.at[c], out_recv.at[c], partner,
        ).wait_recv()


def chained(inputs, upstream, arranged, key_old, key_moment, key_second):
    tokens, width = inputs.shape
    columns = upstream.shape[1]
    half = columns // 2
    chunk = 256 if half % 256 == 0 else 128
    count = half // chunk
    block = width // CHAIN
    groups = arranged.shape[0]
    vmem = pl.BlockSpec(memory_space=pltpu.VMEM)
    hbm = pl.BlockSpec(memory_space=pl.ANY)
    key_shape = jax.ShapeDtypeStruct(key_old.shape, jnp.float32)
    dma = pltpu.SemaphoreType.DMA
    return pl.pallas_call(
        functools.partial(kernel, chunk),
        out_shape=(
            jax.ShapeDtypeStruct((width // (2 * CHAIN), columns), jnp.bfloat16),
            jax.ShapeDtypeStruct((groups,) + key_old.shape, jnp.float32),
            key_shape,
            key_shape,
        ),
        in_specs=[vmem, hbm, vmem, vmem, vmem, vmem],
        out_specs=(hbm, vmem, vmem, vmem),
        scratch_shapes=[
            pltpu.VMEM((width, 4 * tokens), jnp.bfloat16),
            pltpu.VMEM((count, 4 * tokens, chunk), jnp.bfloat16),
            pltpu.VMEM((count, 2 * block, chunk), jnp.bfloat16),
            pltpu.VMEM((count, 2 * block, chunk), jnp.bfloat16),
            pltpu.VMEM((count, block, chunk), jnp.bfloat16),
            pltpu.VMEM((count, block, chunk), jnp.bfloat16),
            pltpu.VMEM((groups - 1,) + key_old.shape, jnp.bfloat16),
        ]
        + [dma((count,))] * 12
        + [dma, dma]
        + [dma((3,))] * 4
        + [dma((groups - 1,))] * 4,
        compiler_params=pltpu.CompilerParams(
            collective_id=0, has_side_effects=True, vmem_limit_bytes=60 * 1024 * 1024
        ),
        cost_estimate=pl.CostEstimate(
            flops=14 * block * block * half, bytes_accessed=4 * width * columns, transcendentals=0
        ),
    )(inputs, upstream, arranged, key_old, key_moment, key_second)


def line_shards(
    expert_inputs,
    hidden_grads,
    expert_weight,
    expert_moment,
    expert_second,
    key_partial,
    key_weight,
    key_moment,
    key_second,
    slice_owner,
):
    groups = lax.axis_size("exp")
    holder = lax.axis_index("exp")
    slice_rows = key_weight.shape[0] // groups
    columns_key = key_weight.shape[1]
    index = jnp.arange(groups, dtype=jnp.int32)

    def pick(mask, blocks):
        return jnp.sum(jnp.where(mask[:, :, None, None], blocks[None], 0.0), axis=1)

    owned = slice_owner[None, :] == index[:, None]
    arranged = pick(owned, key_partial[0].reshape(groups, slice_rows, columns_key))
    held_slice = jnp.sum(jnp.where(slice_owner == holder, index, 0))
    old_slice = lax.dynamic_slice_in_dim(key_weight, held_slice * slice_rows, slice_rows, 0)
    gradient, gathered, key_moment_new, key_second_new = chained(
        expert_inputs[0],
        hidden_grads[0],
        arranged.astype(jnp.bfloat16),
        old_slice,
        key_moment[0],
        key_second[0],
    )
    weight_next, moment_f, second_f = adam_update(
        expert_weight[0], expert_moment[0], expert_second[0], gradient.astype(jnp.float32)
    )
    key_next = pick(owned.T, gathered).reshape(key_weight.shape)
    return (
        weight_next[None],
        moment_f.astype(jnp.bfloat16)[None],
        second_f.astype(jnp.bfloat16)[None],
        key_next,
        key_moment_new[None],
        key_second_new[None],
    )


def solution(mesh):
    in_specs = (
        P("exp", "dp", None),
        P("exp", "dp", None),
        P("exp", "dp", None),
        P("exp", "dp", None),
        P("exp", "dp", None),
        P("exp", "dp", None),
        P("dp", None),
        P("exp", "dp", None),
        P("exp", "dp", None),
        P(),
    )
    out_specs = (
        P("exp", "dp", None),
        P("exp", "dp", None),
        P("exp", "dp", None),
        P("dp", None),
        P("exp", "dp", None),
        P("exp", "dp", None),
    )
    body = line_shards if mesh.shape["dp"] == 2 * CHAIN else shards
    return jax.shard_map(body, mesh=mesh, in_specs=in_specs, out_specs=out_specs, check_vma=False)
```

```python
import functools

import jax
import jax.numpy as jnp
from jax import lax
from jax.experimental import pallas as pl
from jax.experimental.pallas import tpu as pltpu
from jax.sharding import PartitionSpec as P

STEP = 10


first_decay = 0.9
second_decay = 0.999
learn_rate = 0.01
weight_decay = 0.1
epsilon = 1e-08


def adam_update(param, moment, second, gradient):
    moment_new = first_decay * moment.astype(jnp.float32) + (1.0 - first_decay) * gradient
    second_new = (
        second_decay * second.astype(jnp.float32) + (1.0 - second_decay) * gradient * gradient
    )
    moment_scale = learn_rate / (1.0 - first_decay**STEP)
    second_scale = 1.0 / (1.0 - second_decay**STEP)
    param_new = (1.0 - learn_rate * weight_decay) * param - (moment_scale * moment_new) / (
        jnp.sqrt(second_scale * second_new) + epsilon
    )
    return (param_new, moment_new, second_new)


def shards(
    expert_inputs,
    hidden_grads,
    expert_weight,
    expert_moment,
    expert_second,
    key_partial,
    key_weight,
    key_moment,
    key_second,
    slice_owner,
):
    inputs = expert_inputs[0]
    upstream = hidden_grads[0]
    gradient = lax.psum_scatter(
        lax.dot_general(
            inputs, upstream, (((0,), (0,)), ((), ())), preferred_element_type=jnp.float32
        ).astype(jnp.bfloat16),
        "dp",
        scatter_dimension=0,
        tiled=True,
    ).astype(jnp.float32)
    weight_next, moment_f, second_f = adam_update(
        expert_weight[0], expert_moment[0], expert_second[0], gradient
    )
    moment_next = moment_f.astype(jnp.bfloat16)
    second_next = second_f.astype(jnp.bfloat16)
    groups = lax.axis_size("exp")
    holder = lax.axis_index("exp")
    shard_rows = key_weight.shape[0]
    slice_rows = shard_rows // groups
    columns_key = key_weight.shape[1]
    picker = (slice_owner[None, :] == jnp.arange(groups, dtype=jnp.int32)[:, None]).astype(
        jnp.float32
    )
    flat_partial = key_partial[0].reshape(groups, slice_rows * columns_key)
    arranged = jnp.dot(
        picker, flat_partial, precision=lax.Precision.HIGHEST, preferred_element_type=jnp.float32
    )
    key_gradient = (
        lax.psum_scatter(arranged.astype(jnp.bfloat16), "exp", scatter_dimension=0, tiled=True)
        .astype(jnp.float32)
        .reshape(slice_rows, columns_key)
    )
    held_slice = jnp.sum(jnp.where(slice_owner == holder, jnp.arange(groups, dtype=jnp.int32), 0))
    old_slice = lax.dynamic_slice_in_dim(key_weight, held_slice * slice_rows, slice_rows, 0)
    slice_new, key_moment_new, key_second_new = adam_update(
        old_slice, key_moment[0], key_second[0], key_gradient
    )
    gathered = lax.all_gather(slice_new, "exp", axis=0, tiled=True).reshape(
        groups, slice_rows * columns_key
    )
    ordered = jnp.dot(
        picker.T, gathered, precision=lax.Precision.HIGHEST, preferred_element_type=jnp.float32
    )
    key_next = ordered.reshape(shard_rows, columns_key)
    return (
        weight_next[None],
        moment_next[None],
        second_next[None],
        key_next,
        key_moment_new[None],
        key_second_new[None],
    )


MESH = pl.DeviceIdType.MESH
CHAIN = 4


def kernel(
    chunk,
    in_hbm,
    hid_ref,
    kpart_hbm,
    kweight_hbm,
    mask_ref,
    kmom_hbm,
    ksec_hbm,
    g_ref,
    knext_out,
    kmom_out,
    ksec_out,
    lhs,
    rhs,
    prod,
    got,
    fwd,
    own,
    karr_ref,
    kall_ref,
    kgot,
    in_ref,
    kpart_ref,
    kweight_ref,
    kmom_ref,
    ksec_ref,
    load_sem,
    local_sem,
    swap_send,
    swap_recv,
    fact_send,
    fact_recv,
    far_send,
    far_recv,
    near_send,
    near_recv,
    out_sem,
    out_send,
    out_recv,
    lhs_send,
    lhs_recv,
    edge_send,
    edge_recv,
    pass_send,
    pass_recv,
    key_send,
    key_recv,
    all_send,
    all_recv,
):
    exp = lax.axis_index("exp")
    groups = lax.axis_size("exp")
    place = lax.axis_index("dp")
    chip = place // 2
    core = place % 2
    other = 1 - core
    partner = (exp, chip * 2 + other)
    tokens, width = in_ref.shape
    rows = width // (2 * CHAIN)
    block = 2 * rows
    half = hid_ref.shape[1] // 2
    count = half // chunk
    middle = (chip == 1) | (chip == 2)
    outer = (chip // 2) * (CHAIN - 1)
    far = CHAIN - 1 - outer
    inner = 1 + (1 - chip // 2)
    near = 1 + chip // 2
    outer_dev = (exp, outer * 2 + core)
    inner_dev = (exp, inner * 2 + core)
    near_dev = (exp, near * 2 + core)

    def remote(src, dst, send, recv, dev):
        return pltpu.make_async_remote_copy(
            src_ref=src, dst_ref=dst, send_sem=send, recv_sem=recv, device_id=dev,
            device_id_type=MESH,
        )

    def rows_of(which):
        return pl.ds(pl.multiple_of(which * block, block), block)

    def columns(side, c):
        return pl.ds(pl.multiple_of(side * half + c * chunk, chunk), chunk)

    def matmul(which, c, depth):
        return jnp.dot(
            lhs[rows_of(which), 0:depth], rhs[c, 0:depth, :], preferred_element_type=jnp.float32
        )

    def local_copy(c):
        return pltpu.make_async_copy(
            hid_ref.at[:, columns(core, c)], rhs.at[c, pl.ds(0, tokens)], local_sem.at[c]
        )

    def swap_copy(c):
        return remote(
            hid_ref.at[:, columns(other, c)], rhs.at[c, pl.ds(tokens, tokens)],
            swap_send.at[c], swap_recv.at[c], partner,
        )

    def factor_copy(c):
        return remote(
            rhs.at[c, pl.ds(0, 2 * tokens)], rhs.at[c, pl.ds(2 * tokens, 2 * tokens)],
            fact_send.at[c], fact_recv.at[c], near_dev,
        )

    def far_copy(c):
        return remote(
            prod.at[c, pl.ds(0, block)], got.at[c, pl.ds(0, block)],
            far_send.at[c], far_recv.at[c], inner_dev,
        )

    def near_copy(c):
        return remote(
            prod.at[c, pl.ds(block, block)], got.at[c, pl.ds(block, block)],
            near_send.at[c], near_recv.at[c], inner_dev,
        )

    def edge_result(c):
        return remote(
            fwd.at[c], got.at[c, pl.ds(block, block)], far_recv_send(c), near_recv.at[c], outer_dev
        )

    def far_recv_send(c):
        return fact_send.at[c]

    def out_copy(c):
        return pltpu.make_async_copy(
            own.at[c, pl.ds(pl.multiple_of(core * rows, rows), rows)],
            g_ref.at[:, columns(core, c)], out_sem.at[c],
        )

    def out_swap(c):
        return remote(
            own.at[c, pl.ds(pl.multiple_of(other * rows, rows), rows)],
            g_ref.at[:, columns(core, c)], out_send.at[c], out_recv.at[c], partner,
        )

    lhs_swap = remote(
        lhs.at[:, pl.ds(0, tokens)], lhs.at[:, pl.ds(tokens, tokens)],
        lhs_send, lhs_recv, partner,
    )

    def part_of(k):
        return (far, inner, near)[k]

    def edge_copy(k):
        at = rows_of(part_of(k))
        return remote(
            lhs.at[at, pl.ds(0, tokens)], lhs.at[at, pl.ds(2 * tokens, tokens)],
            edge_send.at[k], edge_recv.at[k], near_dev,
        )

    def pass_copy(k):
        at = rows_of(part_of(k))
        return remote(
            lhs.at[at, pl.ds(2 * tokens, tokens)], lhs.at[at, pl.ds(3 * tokens, tokens)],
            pass_send.at[k], pass_recv.at[k], partner,
        )

    def key_copy(d):
        peer = lax.rem(exp + d, groups)
        return remote(
            karr_ref.at[peer], kgot.at[d - 1], key_send.at[d - 1], key_recv.at[d - 1],
            (peer, place),
        )

    def all_copy(d):
        peer = lax.rem(exp + d, groups)
        return remote(
            kall_ref.at[exp], kall_ref.at[exp], all_send.at[d - 1], all_recv.at[d - 1],
            (peer, place),
        )

    def all_arrival(d):
        source = lax.rem(exp + groups - d, groups)
        return remote(
            kall_ref.at[source], kall_ref.at[source], all_send.at[d - 1], all_recv.at[d - 1],
            (source, place),
        )

    slice_rows = kmom_ref.shape[0]

    def picked(ref, holder):
        return sum(
            mask_ref[holder * groups + s] * ref[s * slice_rows : (s + 1) * slice_rows, :]
            for s in range(groups)
        )

    barrier = pltpu.get_barrier_semaphore()

    loads = [
        pltpu.make_async_copy(src, dst, load_sem.at[i])
        for i, (src, dst) in enumerate(
            (
                (in_hbm, in_ref),
                (kpart_hbm, kpart_ref),
                (kweight_hbm, kweight_ref),
                (kmom_hbm, kmom_ref),
                (ksec_hbm, ksec_ref),
            )
        )
    ]
    for load in loads:
        load.start()
    local_copy(0).start()

    def greet(dev):
        pl.semaphore_signal(barrier, inc=1, device_id=dev, device_id_type=MESH)

    greet(partner)
    for d in range(1, groups):
        greet((lax.rem(exp + d, groups), place))

    @pl.when(middle)
    def _():
        greet(outer_dev)
        greet(inner_dev)
        pl.semaphore_wait(barrier, groups + 2)

    @pl.when(jnp.logical_not(middle))
    def _():
        greet(near_dev)
        pl.semaphore_wait(barrier, groups + 1)

    swap_copy(0).start()
    loads[0].wait()

    @pl.loop(0, 2 * CHAIN)
    def _(q):
        at = pl.ds(pl.multiple_of(q * rows, rows), rows)
        lhs[at, 0:tokens] = in_ref[:, at].T

    @pl.when(jnp.logical_not(middle))
    def _():
        edge_copy(0).start()

    lhs_swap.start()

    @pl.loop(1, count)
    def _(c):
        local_copy(c).start()
        swap_copy(c).start()

    for load in loads[1:]:
        load.wait()
    for h in range(groups):
        karr_ref[h] = picked(kpart_ref, h).astype(karr_ref.dtype)
    for d in range(1, groups):
        key_copy(d).start()

    def key_step():
        for d in range(1, groups):
            key_copy(d).wait_recv()
        total = karr_ref[exp].astype(jnp.float32)
        for d in range(1, groups):
            total += kgot[d - 1].astype(jnp.float32)
        old = picked(kweight_ref, exp)
        new, moment, second = adam_update(old, kmom_ref[...], ksec_ref[...], total)
        kmom_out[...] = moment
        ksec_out[...] = second
        kall_ref[exp] = new
        for d in range(1, groups):
            all_copy(d).start()

    def finish(c, depth):
        own[c] = (matmul(chip, c, depth) + got[c, block:, :].astype(jnp.float32)).astype(own.dtype)
        out_copy(c).start()
        out_swap(c).start()

    @pl.when(jnp.logical_not(middle))
    def _():
        @pl.loop(0, count)
        def _(c):
            local_copy(c).wait()
            swap_copy(c).wait_recv()
            factor_copy(c).start()

            @pl.when(c == 0)
            def _():
                edge_copy(1).start()

            @pl.when(c == 2)
            def _():
                edge_copy(2).start()

        lhs_swap.wait_recv()
        key_step()

        @pl.loop(0, count)
        def _(c):
            near_copy(c).wait_recv()
            finish(c, 2 * tokens)

        @pl.loop(0, count)
        def _(c):
            factor_copy(c).wait_send()

        for k in range(3):
            edge_copy(k).wait_send()

    @pl.when(middle)
    def _():
        def take(k):
            edge_copy(k).wait_recv()
            pass_copy(k).start()
            pass_copy(k).wait_recv()

        lhs_swap.wait_recv()
        take(0)

        @pl.loop(0, count + 2)
        def _(c):
            @pl.when(c < count)
            def _():
                local_copy(c).wait()
                swap_copy(c).wait_recv()
                factor_copy(c).wait_recv()
                prod[c, 0:block, :] = matmul(far, c, 4 * tokens).astype(prod.dtype)
                far_copy(c).start()

                @pl.when(c == 0)
                def _():
                    take(1)

                prod[c, block:, :] = matmul(inner, c, 4 * tokens).astype(prod.dtype)
                near_copy(c).start()

            @pl.when(c == 2)
            def _():
                take(2)
                key_step()

            @pl.when(c >= 2)
            def _():
                p = c - 2
                far_copy(p).wait_recv()
                fwd[p] = (
                    matmul(outer, p, 2 * tokens) + got[p, 0:block, :].astype(jnp.float32)
                ).astype(fwd.dtype)
                edge_result(p).start()
                near_copy(p).wait_recv()
                finish(p, 4 * tokens)

        @pl.loop(0, count)
        def _(c):
            far_copy(c).wait_send()
            near_copy(c).wait_send()
            edge_result(c).wait_send()

        for k in range(3):
            pass_copy(k).wait_send()

    lhs_swap.wait_send()
    for d in range(1, groups):
        key_copy(d).wait_send()
        all_copy(d).wait_send()
        all_arrival(d).wait_recv()

    for s in range(groups):
        knext_out[s * slice_rows : (s + 1) * slice_rows, :] = sum(
            mask_ref[h * groups + s] * kall_ref[h] for h in range(groups)
        )

    @pl.loop(0, count)
    def _(c):
        swap_copy(c).wait_send()
        out_copy(c).wait()
        out_swap(c).wait_send()
        remote(
            own.at[c, pl.ds(0, rows)], g_ref.at[:, columns(other, c)],
            out_send.at[c], out_recv.at[c], partner,
        ).wait_recv()


def chained(inputs, upstream, key_partial, key_weight, owner, key_moment, key_second):
    tokens, width = inputs.shape
    columns = upstream.shape[1]
    half = columns // 2
    chunk = 256
    count = half // chunk
    block = width // CHAIN
    groups = owner.shape[0]
    index = jnp.arange(groups, dtype=jnp.int32)
    mask = (owner[None, :] == index[:, None]).astype(jnp.float32).reshape(groups * groups, 1, 1)
    mask = jnp.broadcast_to(mask, (groups * groups, 1, key_weight.shape[1]))
    vmem = pl.BlockSpec(memory_space=pltpu.VMEM)
    hbm = pl.BlockSpec(memory_space=pltpu.HBM)
    key_shape = jax.ShapeDtypeStruct(key_moment.shape, jnp.float32)
    dma = pltpu.SemaphoreType.DMA

    def hold(x):
        return pltpu.with_memory_space_constraint(x, pltpu.HBM)

    return pl.pallas_call(
        functools.partial(kernel, chunk),
        out_shape=(
            jax.ShapeDtypeStruct((width // (2 * CHAIN), columns), jnp.bfloat16),
            jax.ShapeDtypeStruct(key_weight.shape, jnp.float32),
            key_shape,
            key_shape,
        ),
        in_specs=[hbm, hbm, hbm, hbm, vmem, hbm, hbm],
        out_specs=(pl.BlockSpec(memory_space=pl.ANY), vmem, vmem, vmem),
        scratch_shapes=[
            pltpu.VMEM((width, 4 * tokens), jnp.bfloat16),
            pltpu.VMEM((count, 4 * tokens, chunk), jnp.bfloat16),
            pltpu.VMEM((count, 2 * block, chunk), jnp.bfloat16),
            pltpu.VMEM((count, 2 * block, chunk), jnp.bfloat16),
            pltpu.VMEM((count, block, chunk), jnp.bfloat16),
            pltpu.VMEM((count, block, chunk), jnp.bfloat16),
            pltpu.VMEM((groups,) + key_moment.shape, jnp.bfloat16),
            pltpu.VMEM((groups,) + key_moment.shape, jnp.float32),
            pltpu.VMEM((groups - 1,) + key_moment.shape, jnp.bfloat16),
            pltpu.VMEM(inputs.shape, jnp.bfloat16),
            pltpu.VMEM(key_partial.shape, jnp.float32),
            pltpu.VMEM(key_weight.shape, jnp.float32),
            pltpu.VMEM(key_moment.shape, jnp.float32),
            pltpu.VMEM(key_second.shape, jnp.float32),
            dma((5,)),
        ]
        + [dma((count,))] * 12
        + [dma, dma]
        + [dma((3,))] * 4
        + [dma((groups - 1,))] * 4,
        compiler_params=pltpu.CompilerParams(
            collective_id=0, has_side_effects=True, vmem_limit_bytes=38 * 1024 * 1024
        ),
        cost_estimate=pl.CostEstimate(
            flops=14 * block * block * half, bytes_accessed=4 * width * columns, transcendentals=0
        ),
    )(*(hold(x) for x in (inputs, upstream, key_partial, key_weight)), mask, hold(key_moment), hold(key_second))


def line_shards(
    expert_inputs,
    hidden_grads,
    expert_weight,
    expert_moment,
    expert_second,
    key_partial,
    key_weight,
    key_moment,
    key_second,
    slice_owner,
):
    gradient, key_next, key_moment_new, key_second_new = chained(
        expert_inputs[0],
        hidden_grads[0],
        key_partial[0],
        key_weight,
        slice_owner,
        key_moment[0],
        key_second[0],
    )
    weight_next, moment_f, second_f = adam_update(
        expert_weight[0], expert_moment[0], expert_second[0], gradient.astype(jnp.float32)
    )
    return (
        weight_next[None],
        moment_f.astype(jnp.bfloat16)[None],
        second_f.astype(jnp.bfloat16)[None],
        key_next,
        key_moment_new[None],
        key_second_new[None],
    )


def solution(mesh):
    in_specs = (
        P("exp", "dp", None),
        P("exp", "dp", None),
        P("exp", "dp", None),
        P("exp", "dp", None),
        P("exp", "dp", None),
        P("exp", "dp", None),
        P("dp", None),
        P("exp", "dp", None),
        P("exp", "dp", None),
        P(),
    )
    out_specs = (
        P("exp", "dp", None),
        P("exp", "dp", None),
        P("exp", "dp", None),
        P("dp", None),
        P("exp", "dp", None),
        P("exp", "dp", None),
    )
    body = line_shards if mesh.shape["dp"] == 2 * CHAIN else shards
    return jax.shard_map(body, mesh=mesh, in_specs=in_specs, out_specs=out_specs, check_vma=False)
```
